32 devices in a mesh: groups: 2 (over y), gx: 4 (over z), gy: 4 (over x, core).
Axes of the slice: x: 2, y: 2, z: 4, core: 2. Of those that a mesh axis runs over, the one named last changes fastest.
Arguments:
- stored_rows: bfloat16 [320, 16384], P(('groups', 'gy'), 'gx'), parts along dimension 0, may hold values from -6 to 6
- new_rows: bfloat16 [16, 16384], P(('groups', 'gy'), 'gx'), parts along dimension 0, may hold values from -6 to 6
- w_query: bfloat16 [16384, 8192], P('gx', 'gy'), may hold values from -0.046875 to 0.046875
- w_key: bfloat16 [16384, 512], P('gx', 'gy'), may hold values from -0.046875 to 0.046875
- w_value: bfloat16 [16384, 512], P('gx', 'gy'), may hold values from -0.046875 to 0.046875
- w_out: bfloat16 [8192, 16384], P('gy', 'gx'), may hold values from -0.0625 to 0.0625
- kv_cache: bfloat16 [2, 16, 512, 512], P(None, ('groups', 'gx'), None, 'gy'), parts along dimension 1, may hold values from -52 to 52
- cache_len: int32 [16], P(('groups', 'gx')), parts along dimension 0, may hold values from 1 to 512, as said below
- owner: int32 [8], P('groups'), parts along dimension 0, may hold values from 0 to 3, as said below
Outputs:
- mixed: bfloat16 [16, 16384], P(('groups', 'gy'), 'gx'), parts along dimension 0
- rebuilt_key: bfloat16 [8, 40, 512], P(('groups', 'gx'), None, 'gy'), parts along dimension 0
- rebuilt_value: bfloat16 [8, 40, 512], P(('groups', 'gx'), None, 'gy'), parts along dimension 0
The draws below stay inside these ranges and needn't reach their ends.
There are 2 independent parts, one for each index of `groups`. The reference program is written for one: setup_inputs(seed, part) draws one part's arguments, and reference() takes and returns one part's arrays. A program takes and returns all parts, laid end to end along the dimension named above; an argument that names none is the same for every part. Nothing has to cross between parts.
Inputs may be any that keep to these rules, and one draw needn't show every extreme that they name: A permutation: each owner index takes exactly one conversation. Only a row's first cache_len slots hold data; some row has all 512 slots in use.
All inputs are finite; a program needn't handle non-finite values.
Results may differ from the reference program's by a relative error of at most 0.013.
Values may be sent and summed in bfloat16 or wider, within the bound.
A program may use at most 64 MiB of HBM per device.

```python
import math
import jax
import jax.numpy as jnp
from jax import lax

D = 16384
HD = 128
QH = 64
KVH = 4
GROUP = 16
QW = 8192
KVW = 512
L = 512
LC = 40
ROWS_DEV = 2
ROWS = 8
NCONV = 4
STORED = 160


def draw_kv_cache(key, part):
    first_key = jax.random.fold_in(jax.random.fold_in(key, 11), 0)
    shape = (2, ROWS, L, KVW)
    base = jax.random.truncated_normal(first_key, -6.0, 6.0, shape, jnp.float32)
    return base.astype(jnp.bfloat16)


def draw_cache_len(key, part):
    first_key, second_key = jax.random.split(jax.random.fold_in(key, 23))
    lengths = jax.random.randint(first_key, (ROWS,), 1, L + 1)
    chosen = jax.random.randint(second_key, (), 0, ROWS)
    return jnp.where(jnp.arange(ROWS) == chosen, L, lengths).astype(jnp.int32)


def draw_owner(key, part):
    owner_key = jax.random.fold_in(key, 37)
    return jax.random.permutation(owner_key, NCONV).astype(jnp.int32)


def steps_of(key, extent, cuts, smallest, largest):
    factor_of, own = 1.0, jax.random.fold_in(key, 6)
    for dim, parts in cuts:
        steps = jnp.exp(jax.random.uniform(jax.random.fold_in(own, dim), (parts,), jnp.float32, smallest / len(cuts), largest / len(cuts)))
        factor_of = factor_of * jnp.repeat(steps, extent[dim] // parts).reshape([-1 if axis == dim else 1 for axis in range(len(extent))])
    return factor_of


def scatter_about(stream_key, shape, width, reach, cuts=(), kind=jnp.bfloat16):
    level = steps_of(stream_key, shape, cuts, -0.22, 0.18) if cuts else 1.0
    drawn = jax.random.normal(stream_key, shape, jnp.float32) * width * level
    return jnp.minimum(jnp.maximum(drawn, -reach), reach).astype(kind)


def setup_inputs(seed: int = 0, part: int = 0) -> dict:
    seeds = jax.random.split(jax.random.key(seed), 10)
    part_keys = jax.random.split(jax.random.fold_in(seeds[9], part), 10)
    return {
        "stored_rows": scatter_about(part_keys[0], (STORED, D), 1.0, 6.0, ((0, 4), (1, 4))),
        "new_rows": scatter_about(part_keys[1], (ROWS, D), 1.0, 6.0, ((0, 4), (1, 4))),
        "w_query": scatter_about(seeds[2], (D, QW), D ** -0.5, 0.046875, ((0, 4), (1, 4))),
        "w_key": scatter_about(seeds[3], (D, KVW), D ** -0.5, 0.046875, ((0, 4), (1, 4))),
        "w_value": scatter_about(seeds[4], (D, KVW), D ** -0.5, 0.046875, ((0, 4), (1, 4))),
        "w_out": scatter_about(seeds[5], (QW, D), QW ** -0.5, 0.0625, ((0, 4), (1, 4))),
        "kv_cache": draw_kv_cache(jax.random.fold_in(jax.random.fold_in(seeds[9], part), 71), part),
        "cache_len": draw_cache_len(jax.random.fold_in(jax.random.fold_in(seeds[9], part), 71), part),
        "owner": draw_owner(jax.random.fold_in(jax.random.fold_in(seeds[9], part), 71), part),
    }


BASE = 500000.0

def rotate(incoming_values, position):
    half = incoming_values.shape[-1] // 2
    index_row = jnp.arange(half).astype(jnp.float32)
    frequency = jnp.exp(index_row * (-2.0 * math.log(BASE) / incoming_values.shape[-1]))
    angle = position.astype(jnp.float32)[..., None] * frequency
    cosine = jnp.cos(angle)
    sine = jnp.sin(angle)
    first_half = incoming_values[..., :half]
    second_half = incoming_values[..., half:]
    return jnp.concatenate([first_half * cosine - second_half * sine, second_half * cosine + first_half * sine], axis=-1)

def reference(stored_rows, new_rows, w_query, w_key, w_value, w_out, kv_cache, cache_len, owner):
    stored_key = jnp.dot(stored_rows, w_key, preferred_element_type=jnp.float32)
    stored_value = jnp.dot(stored_rows, w_value, preferred_element_type=jnp.float32)
    slot_ids = jnp.arange(NCONV, dtype=jnp.int32)
    inverse = lax.optimization_barrier(jnp.sum(jnp.where(owner[None, :] == slot_ids[:, None], slot_ids[None, :], 0), axis=1)).astype(jnp.int32)
    own_key = stored_key.reshape(NCONV, LC, KVW)[inverse]
    own_value = stored_value.reshape(NCONV, LC, KVW)[inverse]
    first_len = cache_len.reshape(NCONV, ROWS_DEV)[:, 0]
    tail_pos = first_len[:, None] + jnp.arange(LC, dtype=jnp.int32)[None, :]
    rebuilt_key = rotate(own_key.reshape(NCONV, LC, KVH, HD), tail_pos[:, :, None]).reshape(NCONV, LC, KVW).astype(jnp.bfloat16)
    rebuilt_value = own_value.astype(jnp.bfloat16)
    query = jnp.dot(new_rows, w_query, preferred_element_type=jnp.float32)
    fresh_key = jnp.dot(new_rows, w_key, preferred_element_type=jnp.float32)
    fresh_value = jnp.dot(new_rows, w_value, preferred_element_type=jnp.float32)
    resumed = jnp.arange(ROWS, dtype=jnp.int32) % ROWS_DEV == 0
    new_pos = cache_len + jnp.where(resumed, LC, 0).astype(jnp.int32)
    query_rot = rotate(query.reshape(ROWS, QH, HD), new_pos[:, None]).astype(jnp.bfloat16)
    rotary_key_rows = rotate(fresh_key.reshape(ROWS, KVH, HD), new_pos[:, None]).astype(jnp.bfloat16)
    value_new = fresh_value.reshape(ROWS, KVH, HD).astype(jnp.bfloat16)
    score_scaling_factor = 1.0 / math.sqrt(HD)
    grouped_query_heads = query_rot.astype(jnp.float32).reshape(ROWS, KVH, GROUP, HD)
    cached_keys_lookup = kv_cache[0].astype(jnp.float32).reshape(ROWS, L, KVH, HD)
    cache_value = kv_cache[1].astype(jnp.float32).reshape(ROWS, L, KVH, HD)
    row_owner = jnp.arange(ROWS, dtype=jnp.int32) // ROWS_DEV
    tail_key = rebuilt_key.astype(jnp.float32).reshape(NCONV, LC, KVH, HD)[row_owner]
    tail_value = rebuilt_value.astype(jnp.float32).reshape(NCONV, LC, KVH, HD)[row_owner]
    live_row_mask = jnp.arange(L, dtype=jnp.int32)[None, :] < cache_len[:, None]
    s_cache = jnp.einsum('bkgd,blkd->bkgl', grouped_query_heads, cached_keys_lookup) * score_scaling_factor
    s_cache = jnp.where(live_row_mask[:, None, None, :], s_cache, -jnp.inf)
    s_tail = jnp.einsum('bkgd,btkd->bkgt', grouped_query_heads, tail_key) * score_scaling_factor
    s_tail = jnp.where(resumed[:, None, None, None], s_tail, -jnp.inf)
    self_score = jnp.einsum('hzrt,hzt->hzr', grouped_query_heads, rotary_key_rows.astype(jnp.float32)) * score_scaling_factor
    highest = jnp.maximum(jnp.maximum(lax.optimization_barrier(jnp.max(s_cache, axis=-1)), lax.optimization_barrier(jnp.max(s_tail, axis=-1))), self_score)
    e_cache = jnp.exp(s_cache - highest[..., None])
    e_tail = jnp.exp(s_tail - highest[..., None])
    e_self = jnp.exp(self_score - highest)
    denominator = lax.optimization_barrier(jnp.sum(e_cache, axis=-1)) + lax.optimization_barrier(jnp.sum(e_tail, axis=-1)) + e_self
    w_cache = (e_cache / denominator[..., None]).astype(jnp.bfloat16)
    w_tail = (e_tail / denominator[..., None]).astype(jnp.bfloat16)
    w_self = (e_self / denominator).astype(jnp.bfloat16)
    attn = jnp.einsum('bkgl,blkd->bkgd', w_cache.astype(jnp.float32), cache_value)
    attn = attn + jnp.einsum('bkgt,btkd->bkgd', w_tail.astype(jnp.float32), tail_value)
    attn = attn + w_self.astype(jnp.float32)[..., None] * value_new.astype(jnp.float32)[:, :, None, :]
    attn = attn.reshape(ROWS, QW).astype(jnp.bfloat16)
    mixed = jnp.dot(attn, w_out, preferred_element_type=jnp.float32).astype(jnp.bfloat16)
    return (mixed, rebuilt_key, rebuilt_value)
```

```python
import functools
import math

import jax
import jax.numpy as jnp
from jax import lax
from jax.experimental import pallas as pl
from jax.experimental.pallas import tpu as pltpu
from jax.sharding import PartitionSpec as P

HD = 128
LC = 40
TAIL = 48
PAD = 128
ROWS_DEV = 2
BASE = 500000.0
F32 = jnp.float32
BF16 = jnp.bfloat16
MESH = pl.DeviceIdType.MESH


def rope_tables(first_position, rows):
    lane = lax.broadcasted_iota(jnp.int32, (rows, HD), 1)
    row = lax.broadcasted_iota(jnp.int32, (rows, HD), 0)
    index = jnp.where(lane < HD // 2, lane, lane - HD // 2).astype(F32)
    frequency = jnp.exp(index * (-2.0 * math.log(BASE) / HD))
    angle = (row + first_position).astype(F32) * frequency
    sine = jnp.sin(angle)
    return jnp.cos(angle), jnp.where(lane < HD // 2, -sine, sine)


def rope(values, cosine, sine):
    return values * cosine + pltpu.roll(values, HD // 2, 1) * sine


def dot(a, b):
    return jnp.dot(a, b, preferred_element_type=F32)


def layer_kernel(
    nx, ny,
    len_ref, owner_ref, stored_ref, new_ref, wq_ref, wk_ref, wv_ref, wo_ref, kv_ref,
    mixed_ref, rkey_ref, rvalue_ref,
    wq, wkv, wo, stored, new, lhs, kv, q_acc, q_out, q_in, part, kv_out, kv_in,
    attn_all, o_out, o_in,
    wq_sem, wkv_sem, wo_sem, kv_sem, own_sem, new_local_sem,
    new_send, new_recv, st_send, st_recv, q_send, q_recv, kvp_send, kvp_recv,
    at_send, at_recv, o_send, o_recv,
):
    x = lax.axis_index("gx")
    y = lax.axis_index("gy")
    features = wq_ref.shape[0]
    qcols = wq_ref.shape[1]
    kcols = wk_ref.shape[1]
    heads = qcols // HD
    slots = kv_ref.shape[2]
    nq = wq_sem.shape[0]
    kc = features // nq
    wo_rows = wo_ref.shape[0] // nq
    nst = own_sem.shape[0]
    fc = features // nst
    conv_here = stored_ref.shape[0] // LC
    rows_here = new_ref.shape[0]
    rows = rows_here * ny
    width = wo_ref.shape[1]
    halves = o_send.shape[1]

    def wq_copy(i):
        r = pl.ds(pl.multiple_of(i * kc, kc), kc)
        return pltpu.make_async_copy(wq_ref.at[r, :], wq.at[r, :], wq_sem.at[i])

    def wo_copy(i):
        r = pl.ds(pl.multiple_of(i * wo_rows, wo_rows), wo_rows)
        return pltpu.make_async_copy(wo_ref.at[r, :], wo.at[r, :], wo_sem.at[i])

    def st_own(j):
        return pltpu.make_async_copy(
            stored_ref.at[:, pl.ds(j * fc, fc)], stored.at[y, :, pl.ds(j * fc, fc)], own_sem.at[j]
        )

    wk_copy = pltpu.make_async_copy(wk_ref, wkv.at[:, pl.ds(0, kcols)], wkv_sem.at[0])
    wv_copy = pltpu.make_async_copy(wv_ref, wkv.at[:, pl.ds(kcols, kcols)], wkv_sem.at[1])
    new_own = pltpu.make_async_copy(new_ref, new.at[y], new_local_sem.at[0])
    kv_copy = pltpu.make_async_copy(kv_ref, kv.at[:, :, pl.ds(0, slots), :], kv_sem.at[0])

    new_own.start()
    for i in range(nq):
        wq_copy(i).start()
    wk_copy.start()
    wv_copy.start()
    for j in range(nst):
        st_own(j).start()
    kv_copy.start()

    barrier = pltpu.get_barrier_semaphore()
    for d in range(1, nx):
        pl.semaphore_signal(
            barrier, inc=1, device_id={"gx": lax.rem(x + d, nx)}, device_id_type=MESH
        )
    for d in range(1, ny):
        pl.semaphore_signal(
            barrier, inc=1, device_id={"gy": lax.rem(y + d, ny)}, device_id_type=MESH
        )
    pl.semaphore_wait(barrier, nx + ny - 2)

    pair = y + 1 - 2 * lax.rem(y, 2)
    cross = lax.rem(y + 2, ny)
    far = 3 - y

    def over_gy(src, dst, ssem, rsem, target):
        return pltpu.make_async_remote_copy(
            src_ref=src, dst_ref=dst, send_sem=ssem, recv_sem=rsem,
            device_id={"gy": target}, device_id_type=MESH,
        )

    def over_gx(src, dst, ssem, rsem, target):
        return pltpu.make_async_remote_copy(
            src_ref=src, dst_ref=dst, send_sem=ssem, recv_sem=rsem,
            device_id={"gx": target}, device_id_type=MESH,
        )

    new_copies = [
        over_gy(new_ref, new.at[y], new_send.at[d], new_recv.at[d], lax.rem(y + d, ny))
        for d in range(1, ny)
    ]
    for c in new_copies:
        c.start()

    def st_copy(kind, j):
        cols = pl.ds(j * fc, fc)
        if kind == 2:
            return over_gy(
                stored.at[cross, :, cols], stored.at[cross, :, cols],
                st_send.at[2, j], st_recv.at[2, j], pair,
            )
        return over_gy(
            stored_ref.at[:, cols], stored.at[y, :, cols],
            st_send.at[kind, j], st_recv.at[kind, j], cross if kind == 1 else pair,
        )

    for kind in (1, 0):
        for j in range(nst):
            st_copy(kind, j).start()

    first_len = len_ref[0]
    cos0, sin0 = rope_tables(first_len, TAIL)
    cos1, sin1 = rope_tables(len_ref[1], 8)
    zeros = jnp.zeros((PAD - TAIL, kcols), BF16)
    for which in range(2):
        for b in range(ROWS_DEV):
            kv[which, b, pl.ds(slots + TAIL, PAD - TAIL), :] = zeros
    q_acc[...] = jnp.zeros_like(q_acc)

    new_own.wait()
    for c in new_copies:
        c.wait_recv()
    lhs[...] = jnp.concatenate([new[s].astype(F32) for s in range(ny)], axis=0).astype(BF16)

    def q_step(i, carry):
        wq_copy(i).wait()
        wo_copy(i).start()
        k = pl.ds(pl.multiple_of(i * kc, kc), kc)
        q_acc[...] += dot(lhs[:, k], wq[k, :])
        return carry

    lax.fori_loop(0, nq, q_step, 0)
    wk_copy.wait()
    wv_copy.wait()
    fresh = dot(lhs[...], wkv[...])
    for o in range(nx):
        r = slice(o * ROWS_DEV, (o + 1) * ROWS_DEV)
        q_out[o, :, pl.ds(0, qcols)] = q_acc[r, :]
        q_out[o, :, pl.ds(qcols, 2 * kcols)] = fresh[r, :]
    q_copies = []
    for d in range(1, nx):
        t = lax.rem(x + d, nx)
        c = over_gx(q_out.at[t], q_in.at[x], q_send.at[d], q_recv.at[d], t)
        c.start()
        q_copies.append(c)

    def project(source, arrive):
        total = None
        for j in range(nst):
            arrive(j)
            cols = pl.ds(j * fc, fc)
            piece = dot(stored[source, :, cols], wkv[cols, :])
            total = piece if total is None else total + piece
        for c in range(conv_here):
            part[source * conv_here + c] = total[c * LC : (c + 1) * LC, :]

    def arrive_cross(j):
        st_copy(1, j).wait_recv()
        st_copy(2, j).start()

    project(y, lambda j: st_own(j).wait())
    project(pair, lambda j: st_copy(0, j).wait_recv())
    project(cross, arrive_cross)
    project(far, lambda j: st_copy(2, j).wait_recv())

    def conversation_of(o):
        def step(c, found):
            return jnp.where(owner_ref[c] == o, c, found)
        return lax.fori_loop(0, nx, step, jnp.int32(0), unroll=nx <= 8)

    for o in range(nx):
        kv_out[o] = part[conversation_of(o)].astype(BF16)
    kvp_copies = []
    for d in range(1, nx):
        t = lax.rem(x + d, nx)
        c = over_gx(kv_out.at[t], kv_in.at[x], kvp_send.at[d], kvp_recv.at[d], t)
        c.start()
        kvp_copies.append(c)

    q_sum = q_out[x]
    for d in range(1, nx):
        q_copies[d - 1].wait_recv()
        q_sum = q_sum + q_in[lax.rem(x + nx - d, nx)]
    scale = 1.0 / math.sqrt(HD)
    at = lax.broadcasted_iota(jnp.int32, (1, slots + PAD), 1)
    tail_row = lax.broadcasted_iota(jnp.int32, (TAIL, kcols), 0)
    kv_copy.wait()

    def query_of(b, cosine, sine):
        stacked = jnp.concatenate(
            [q_sum[b : b + 1, h * HD : (h + 1) * HD] for h in range(heads)], axis=0
        )
        return rope(stacked, cosine, sine).astype(BF16)

    def attend(b, query, live):
        s = lax.dot_general(
            query, kv[0, b], (((1,), (1,)), ((), ())), preferred_element_type=F32
        ) * scale
        s = jnp.where(live, s, -jnp.inf)
        e = jnp.exp(s - jnp.max(s, axis=1, keepdims=True))
        w = (e / jnp.sum(e, axis=1, keepdims=True)).astype(BF16)
        return dot(w, kv[1, b])

    key1 = rope(q_sum[1:2, qcols : qcols + kcols], cos1[0:1], sin1[0:1])
    value1 = q_sum[1:2, qcols + kcols :]
    tail = pl.ds(slots, TAIL)
    kv[0, 1, tail, :] = jnp.where(tail_row == LC, key1, 0.0).astype(BF16)
    kv[1, 1, tail, :] = jnp.where(tail_row == LC, value1, 0.0).astype(BF16)
    attn1 = attend(1, query_of(1, cos1[0:1], sin1[0:1]), (at < len_ref[1]) | (at == slots + LC))
    query0 = query_of(0, cos0[LC : LC + 1], sin0[LC : LC + 1])

    kv_sum = part[conversation_of(x)]
    for d in range(1, nx):
        kvp_copies[d - 1].wait_recv()
        kv_sum = kv_sum + kv_in[lax.rem(x + nx - d, nx)].astype(F32)
    rest = jnp.zeros((TAIL - LC - 1, kcols), F32)
    key0 = jnp.concatenate([kv_sum[:, :kcols], q_sum[0:1, qcols : qcols + kcols], rest], axis=0)
    value0 = jnp.concatenate([kv_sum[:, kcols:], q_sum[0:1, qcols + kcols :], rest], axis=0)
    key0 = rope(key0, cos0, sin0).astype(BF16)
    value0 = value0.astype(BF16)
    kv[0, 0, tail, :] = key0
    kv[1, 0, tail, :] = value0
    rkey_ref[0] = key0[:LC]
    rvalue_ref[0] = value0[:LC]
    attn0 = attend(0, query0, (at < first_len) | ((at >= slots) & (at <= slots + LC)))

    attn_all[x] = jnp.concatenate(
        [
            jnp.concatenate([a[h : h + 1, :] for h in range(heads)], axis=1)
            for a in (attn0, attn1)
        ],
        axis=0,
    ).astype(BF16)
    at_copies = []
    for d in range(1, nx):
        c = over_gx(
            attn_all.at[x], attn_all.at[x], at_send.at[d], at_recv.at[d], lax.rem(x + d, nx)
        )
        c.start()
        at_copies.append(c)
    for i in range(nq):
        wo_copy(i).wait()
    for c in at_copies:
        c.wait_recv()
    attn = jnp.concatenate([attn_all[s].astype(F32) for s in range(nx)], axis=0).astype(BF16)

    half = width // halves
    cw = min(512, half)
    o_copies = []
    for h in range(halves):
        def o_step(i, carry):
            cols = pl.ds(pl.multiple_of(h * half + i * cw, cw), cw)
            piece = dot(attn, wo[:, cols])
            for g in range(ny):
                o_out[g, :, cols] = piece[g * rows_here : (g + 1) * rows_here].astype(BF16)
            return carry

        lax.fori_loop(0, half // cw, o_step, 0)
        cols = pl.ds(h * half, half)
        for d in range(1, ny):
            t = lax.rem(y + d, ny)
            c = over_gy(
                o_out.at[t, :, cols], o_in.at[y, :, cols], o_send.at[d, h], o_recv.at[d, h], t
            )
            c.start()
            o_copies.append(c)
    for h in range(halves):
        cols = pl.ds(h * half, half)
        total = o_out[y, :, cols].astype(F32)
        for d in range(1, ny):
            o_copies[h * (ny - 1) + d - 1].wait_recv()
            total = total + o_in[lax.rem(y + ny - d, ny), :, cols].astype(F32)
        mixed_ref[:, cols] = total.astype(BF16)

    for c in new_copies + q_copies + kvp_copies + at_copies + o_copies:
        c.wait_send()
    for kind in range(3):
        for j in range(nst):
            st_copy(kind, j).wait_send()


def per_device(stored_rows, new_rows, w_query, w_key, w_value, w_out, kv_cache, cache_len, owner):
    nx, ny = lax.axis_size("gx"), lax.axis_size("gy")
    features, qcols = w_query.shape
    kcols = w_key.shape[1]
    width = w_out.shape[1]
    slots = kv_cache.shape[2]
    rows_here = new_rows.shape[0]
    rows = rows_here * ny
    nq = max(1, features // 512)
    nst = max(1, features // 1024)
    halves = 2 if width >= 1024 else 1
    dma = pltpu.SemaphoreType.DMA
    hbm = pl.BlockSpec(memory_space=pl.ANY)
    smem = pl.BlockSpec(memory_space=pltpu.SMEM)
    vmem = pl.BlockSpec(memory_space=pltpu.VMEM)
    return pl.pallas_call(
        functools.partial(layer_kernel, nx, ny),
        out_shape=(
            jax.ShapeDtypeStruct((rows_here, width), BF16),
            jax.ShapeDtypeStruct((1, LC, kcols), BF16),
            jax.ShapeDtypeStruct((1, LC, kcols), BF16),
        ),
        in_specs=[smem, smem] + [hbm] * 7,
        out_specs=(vmem, vmem, vmem),
        scratch_shapes=[
            pltpu.VMEM(w_query.shape, BF16),
            pltpu.VMEM((features, 2 * kcols), BF16),
            pltpu.VMEM(w_out.shape, BF16),
            pltpu.VMEM((ny,) + stored_rows.shape, BF16),
            pltpu.VMEM((ny,) + new_rows.shape, BF16),
            pltpu.VMEM((rows, features), BF16),
            pltpu.VMEM((2, ROWS_DEV, slots + PAD, kcols), BF16),
            pltpu.VMEM((rows, qcols), F32),
            pltpu.VMEM((nx, ROWS_DEV, qcols + 2 * kcols), F32),
            pltpu.VMEM((nx, ROWS_DEV, qcols + 2 * kcols), F32),
            pltpu.VMEM((nx, LC, 2 * kcols), F32),
            pltpu.VMEM((nx, LC, 2 * kcols), BF16),
            pltpu.VMEM((nx, LC, 2 * kcols), BF16),
            pltpu.VMEM((nx, ROWS_DEV, qcols), BF16),
            pltpu.VMEM((ny, rows_here, width), BF16),
            pltpu.VMEM((ny, rows_here, width), BF16),
            dma((nq,)), dma((2,)), dma((nq,)), dma((1,)), dma((nst,)), dma((1,)),
            dma((ny,)), dma((ny,)), dma((3, nst)), dma((3, nst)),
            dma((nx,)), dma((nx,)), dma((nx,)), dma((nx,)),
            dma((nx,)), dma((nx,)), dma((ny, halves)), dma((ny, halves)),
        ],
        compiler_params=pltpu.CompilerParams(
            collective_id=0, has_side_effects=True, vmem_limit_bytes=60 * 1024 * 1024
        ),
    )(cache_len, owner, stored_rows, new_rows, w_query, w_key, w_value, w_out, kv_cache)


def solution(mesh):
    in_specs = (
        P(("groups", "gy"), "gx"),
        P(("groups", "gy"), "gx"),
        P("gx", "gy"),
        P("gx", "gy"),
        P("gx", "gy"),
        P("gy", "gx"),
        P(None, ("groups", "gx"), None, "gy"),
        P(("groups", "gx")),
        P("groups"),
    )
    out_specs = (
        P(("groups", "gy"), "gx"),
        P(("groups", "gx"), None, "gy"),
        P(("groups", "gx"), None, "gy"),
    )
    return jax.shard_map(
        per_device, mesh=mesh, in_specs=in_specs, out_specs=out_specs, check_vma=False
    )
```

```python
import functools
import math

import jax
import jax.numpy as jnp
from jax import lax
from jax.experimental import pallas as pl
from jax.experimental.pallas import tpu as pltpu
from jax.sharding import PartitionSpec as P

HD = 128
LC = 40
TAIL = 48
PAD = 128
ROWS_DEV = 2
BASE = 500000.0
F32 = jnp.float32
BF16 = jnp.bfloat16
MESH = pl.DeviceIdType.MESH


def rope_tables(first_position, rows):
    lane = lax.broadcasted_iota(jnp.int32, (rows, HD), 1)
    row = lax.broadcasted_iota(jnp.int32, (rows, HD), 0)
    index = jnp.where(lane < HD // 2, lane, lane - HD // 2).astype(F32)
    frequency = jnp.exp(index * (-2.0 * math.log(BASE) / HD))
    angle = (row + first_position).astype(F32) * frequency
    sine = jnp.sin(angle)
    return jnp.cos(angle), jnp.where(lane < HD // 2, -sine, sine)


def rope(values, cosine, sine):
    return values * cosine + pltpu.roll(values, HD // 2, 1) * sine


def dot(a, b):
    return jnp.dot(a, b, preferred_element_type=F32)


def layer_kernel(
    nx, ny,
    len_ref, owner_ref, stored_ref, new_ref, wq_ref, wk_ref, wv_ref, wo_ref, kv_ref,
    mixed_ref, rkey_ref, rvalue_ref,
    wq, wkv, wo, stored, new, lhs, kv, q_acc, q_out, q_in, part, kv_out, kv_in,
    attn_all, o_out, o_in,
    wq_sem, wkv_sem, wo_sem, kv_sem, own_sem, new_local_sem,
    new_send, new_recv, st_send, st_recv, q_send, q_recv, kvp_send, kvp_recv,
    at_send, at_recv, o_send, o_recv,
):
    x = lax.axis_index("gx")
    y = lax.axis_index("gy")
    features = wq_ref.shape[0]
    qcols = wq_ref.shape[1]
    kcols = wk_ref.shape[1]
    heads = qcols // HD
    slots = kv_ref.shape[2]
    nq = wq_sem.shape[0]
    kc = features // nq
    wo_rows = wo_ref.shape[0] // nq
    nst = own_sem.shape[0]
    fc = features // nst
    conv_here = stored_ref.shape[0] // LC
    rows_here = new_ref.shape[0]
    rows = rows_here * ny
    width = wo_ref.shape[1]
    halves = o_send.shape[1]

    def wq_copy(i):
        r = pl.ds(pl.multiple_of(i * kc, kc), kc)
        return pltpu.make_async_copy(wq_ref.at[r, :], wq.at[r, :], wq_sem.at[i])

    def wo_copy(i):
        r = pl.ds(pl.multiple_of(i * wo_rows, wo_rows), wo_rows)
        return pltpu.make_async_copy(wo_ref.at[r, :], wo.at[r, :], wo_sem.at[i])

    def st_own(j):
        return pltpu.make_async_copy(
            stored_ref.at[:, pl.ds(j * fc, fc)], stored.at[y, :, pl.ds(j * fc, fc)], own_sem.at[j]
        )

    wk_copy = pltpu.make_async_copy(wk_ref, wkv.at[:, pl.ds(0, kcols)], wkv_sem.at[0])
    wv_copy = pltpu.make_async_copy(wv_ref, wkv.at[:, pl.ds(kcols, kcols)], wkv_sem.at[1])
    new_own = pltpu.make_async_copy(new_ref, new.at[y], new_local_sem.at[0])
    kv_copy = pltpu.make_async_copy(kv_ref, kv.at[:, :, pl.ds(0, slots), :], kv_sem.at[0])

    new_own.start()
    for i in range(nq):
        wq_copy(i).start()
    wk_copy.start()
    wv_copy.start()
    for j in range(nst):
        st_own(j).start()
    kv_copy.start()

    barrier = pltpu.get_barrier_semaphore()
    for d in range(1, nx):
        pl.semaphore_signal(
            barrier, inc=1, device_id={"gx": lax.rem(x + d, nx)}, device_id_type=MESH
        )
    for d in range(1, ny):
        pl.semaphore_signal(
            barrier, inc=1, device_id={"gy": lax.rem(y + d, ny)}, device_id_type=MESH
        )
    pl.semaphore_wait(barrier, nx + ny - 2)

    pair = y + 1 - 2 * lax.rem(y, 2)
    cross = lax.rem(y + 2, ny)
    far = 3 - y

    def over_gy(src, dst, ssem, rsem, target):
        return pltpu.make_async_remote_copy(
            src_ref=src, dst_ref=dst, send_sem=ssem, recv_sem=rsem,
            device_id={"gy": target}, device_id_type=MESH,
        )

    def over_gx(src, dst, ssem, rsem, target):
        return pltpu.make_async_remote_copy(
            src_ref=src, dst_ref=dst, send_sem=ssem, recv_sem=rsem,
            device_id={"gx": target}, device_id_type=MESH,
        )

    new_copies = [
        over_gy(new_ref, new.at[y], new_send.at[d], new_recv.at[d], lax.rem(y + d, ny))
        for d in range(1, ny)
    ]
    for c in new_copies:
        c.start()

    def st_copy(kind, j):
        cols = pl.ds(j * fc, fc)
        if kind == 2:
            return over_gy(
                stored.at[cross, :, cols], stored.at[cross, :, cols],
                st_send.at[2, j], st_recv.at[2, j], pair,
            )
        return over_gy(
            stored_ref.at[:, cols], stored.at[y, :, cols],
            st_send.at[kind, j], st_recv.at[kind, j], cross if kind == 1 else pair,
        )

    for kind in (1, 0):
        for j in range(nst):
            st_copy(kind, j).start()

    first_len = len_ref[0]
    cos0, sin0 = rope_tables(first_len, TAIL)
    cos1, sin1 = rope_tables(len_ref[1], 8)
    zeros = jnp.zeros((PAD - TAIL, kcols), BF16)
    for which in range(2):
        kv[which, 1, pl.ds(slots + TAIL, PAD - TAIL), :] = zeros
    q_acc[...] = jnp.zeros_like(q_acc)

    new_own.wait()
    for c in new_copies:
        c.wait_recv()
    lhs[...] = jnp.concatenate([new[s].astype(F32) for s in range(ny)], axis=0).astype(BF16)

    def q_step(i, carry):
        wq_copy(i).wait()
        wo_copy(i).start()
        k = pl.ds(pl.multiple_of(i * kc, kc), kc)
        q_acc[...] += dot(lhs[:, k], wq[k, :])
        return carry

    lax.fori_loop(0, nq, q_step, 0)
    wk_copy.wait()
    wv_copy.wait()
    fresh = dot(lhs[...], wkv[...])
    for o in range(nx):
        r = slice(o * ROWS_DEV, (o + 1) * ROWS_DEV)
        q_out[o, :, pl.ds(0, qcols)] = q_acc[r, :]
        q_out[o, :, pl.ds(qcols, 2 * kcols)] = fresh[r, :]
    q_copies = []
    for d in range(1, nx):
        t = lax.rem(x + d, nx)
        c = over_gx(q_out.at[t], q_in.at[x], q_send.at[d], q_recv.at[d], t)
        c.start()
        q_copies.append(c)

    def project(source, arrive):
        total = None
        for j in range(nst):
            arrive(j)
            cols = pl.ds(j * fc, fc)
            piece = dot(stored[source, :, cols], wkv[cols, :])
            total = piece if total is None else total + piece
        for c in range(conv_here):
            part[source * conv_here + c] = total[c * LC : (c + 1) * LC, :]

    def arrive_cross(j):
        st_copy(1, j).wait_recv()
        st_copy(2, j).start()

    project(y, lambda j: st_own(j).wait())
    project(pair, lambda j: st_copy(0, j).wait_recv())
    project(cross, arrive_cross)
    project(far, lambda j: st_copy(2, j).wait_recv())

    def conversation_of(o):
        def step(c, found):
            return jnp.where(owner_ref[c] == o, c, found)
        return lax.fori_loop(0, nx, step, jnp.int32(0), unroll=nx <= 8)

    for o in range(nx):
        kv_out[o] = part[conversation_of(o)].astype(BF16)
    kvp_copies = []
    for d in range(1, nx):
        t = lax.rem(x + d, nx)
        c = over_gx(kv_out.at[t], kv_in.at[x], kvp_send.at[d], kvp_recv.at[d], t)
        c.start()
        kvp_copies.append(c)

    q_sum = q_out[x]
    for d in range(1, nx):
        q_copies[d - 1].wait_recv()
        q_sum = q_sum + q_in[lax.rem(x + nx - d, nx)]
    scale = 1.0 / math.sqrt(HD)
    at = lax.broadcasted_iota(jnp.int32, (1, slots + PAD), 1)
    tail_row = lax.broadcasted_iota(jnp.int32, (TAIL, kcols), 0)
    kv_copy.wait()

    def query_of(b, cosine, sine):
        stacked = jnp.concatenate(
            [q_sum[b : b + 1, h * HD : (h + 1) * HD] for h in range(heads)], axis=0
        )
        return rope(stacked, cosine, sine).astype(BF16)

    def scores(query, keys):
        return lax.dot_general(
            query, keys, (((1,), (1,)), ((), ())), preferred_element_type=F32
        ) * scale

    def attend(b, query, live):
        s = jnp.where(live, scores(query, kv[0, b]), -jnp.inf)
        e = jnp.exp(s - jnp.max(s, axis=1, keepdims=True))
        w = (e / jnp.sum(e, axis=1, keepdims=True)).astype(BF16)
        return dot(w, kv[1, b])

    key1 = rope(q_sum[1:2, qcols : qcols + kcols], cos1[0:1], sin1[0:1])
    value1 = q_sum[1:2, qcols + kcols :]
    tail = pl.ds(slots, TAIL)
    kv[0, 1, tail, :] = jnp.where(tail_row == LC, key1, 0.0).astype(BF16)
    kv[1, 1, tail, :] = jnp.where(tail_row == LC, value1, 0.0).astype(BF16)
    attn1 = attend(1, query_of(1, cos1[0:1], sin1[0:1]), (at < len_ref[1]) | (at == slots + LC))
    query0 = query_of(0, cos0[LC : LC + 1], sin0[LC : LC + 1])
    cached0 = jnp.where(at[:, :slots] < first_len, scores(query0, kv[0, 0, :slots]), -jnp.inf)
    cached_top = jnp.max(cached0, axis=1, keepdims=True)

    kv_sum = part[conversation_of(x)]
    for d in range(1, nx):
        kvp_copies[d - 1].wait_recv()
        kv_sum = kv_sum + kv_in[lax.rem(x + nx - d, nx)].astype(F32)
    rest = jnp.zeros((TAIL - LC - 1, kcols), F32)
    key0 = jnp.concatenate([kv_sum[:, :kcols], q_sum[0:1, qcols : qcols + kcols], rest], axis=0)
    value0 = jnp.concatenate([kv_sum[:, kcols:], q_sum[0:1, qcols + kcols :], rest], axis=0)
    key0 = rope(key0, cos0, sin0).astype(BF16)
    value0 = value0.astype(BF16)
    tail0 = jnp.where(
        lax.broadcasted_iota(jnp.int32, (1, TAIL), 1) <= LC, scores(query0, key0), -jnp.inf
    )
    top = jnp.maximum(cached_top, jnp.max(tail0, axis=1, keepdims=True))
    e_cached = jnp.exp(cached0 - top)
    e_tail = jnp.exp(tail0 - top)
    total = jnp.sum(e_cached, axis=1, keepdims=True) + jnp.sum(e_tail, axis=1, keepdims=True)
    attn0 = dot((e_cached / total).astype(BF16), kv[1, 0, :slots])
    attn0 = attn0 + dot((e_tail / total).astype(BF16), value0)

    attn_all[x] = jnp.concatenate(
        [
            jnp.concatenate([a[h : h + 1, :] for h in range(heads)], axis=1)
            for a in (attn0, attn1)
        ],
        axis=0,
    ).astype(BF16)
    at_copies = []
    for d in range(1, nx):
        c = over_gx(
            attn_all.at[x], attn_all.at[x], at_send.at[d], at_recv.at[d], lax.rem(x + d, nx)
        )
        c.start()
        at_copies.append(c)
    rkey_ref[0] = key0[:LC]
    rvalue_ref[0] = value0[:LC]
    for i in range(nq):
        wo_copy(i).wait()
    for c in at_copies:
        c.wait_recv()
    attn = jnp.concatenate([attn_all[s].astype(F32) for s in range(nx)], axis=0).astype(BF16)

    half = width // halves
    cw = min(512, half)
    o_copies = []
    for h in range(halves):
        def o_step(i, carry):
            cols = pl.ds(pl.multiple_of(h * half + i * cw, cw), cw)
            piece = dot(attn, wo[:, cols])
            for g in range(ny):
                o_out[g, :, cols] = piece[g * rows_here : (g + 1) * rows_here].astype(BF16)
            return carry

        lax.fori_loop(0, half // cw, o_step, 0)
        cols = pl.ds(h * half, half)
        for d in range(1, ny):
            t = lax.rem(y + d, ny)
            c = over_gy(
                o_out.at[t, :, cols], o_in.at[y, :, cols], o_send.at[d, h], o_recv.at[d, h], t
            )
            c.start()
            o_copies.append(c)
    for h in range(halves):
        cols = pl.ds(h * half, half)
        total = o_out[y, :, cols].astype(F32)
        for d in range(1, ny):
            o_copies[h * (ny - 1) + d - 1].wait_recv()
            total = total + o_in[lax.rem(y + ny - d, ny), :, cols].astype(F32)
        mixed_ref[:, cols] = total.astype(BF16)

    for c in new_copies + q_copies + kvp_copies + at_copies + o_copies:
        c.wait_send()
    for kind in range(3):
        for j in range(nst):
            st_copy(kind, j).wait_send()


def hand_over(*refs):
    sources, results, held = refs[:3], refs[3:6], refs[6:9]
    arrive, leave = refs[9:]
    taken = [pltpu.make_async_copy(sources[i], held[i], arrive.at[i]) for i in range(3)]
    given = [pltpu.make_async_copy(held[i], results[i], leave.at[i]) for i in range(3)]
    for c in taken:
        c.start()
    for t, g in zip(taken, given):
        t.wait()
        g.start()
    for g in given:
        g.wait()


def per_device(stored_rows, new_rows, w_query, w_key, w_value, w_out, kv_cache, cache_len, owner):
    nx, ny = lax.axis_size("gx"), lax.axis_size("gy")
    features, qcols = w_query.shape
    kcols = w_key.shape[1]
    width = w_out.shape[1]
    slots = kv_cache.shape[2]
    rows_here = new_rows.shape[0]
    rows = rows_here * ny
    nq = max(1, features // 512)
    nst = max(1, features // 1024)
    halves = max(1, width // 2048)
    dma = pltpu.SemaphoreType.DMA
    hbm = pl.BlockSpec(memory_space=pltpu.HBM)
    smem = pl.BlockSpec(memory_space=pltpu.SMEM)
    vmem = pl.BlockSpec(memory_space=pltpu.VMEM)
    out_shape = (
        jax.ShapeDtypeStruct((rows_here, width), BF16),
        jax.ShapeDtypeStruct((1, LC, kcols), BF16),
        jax.ShapeDtypeStruct((1, LC, kcols), BF16),
    )
    results = pl.pallas_call(
        functools.partial(layer_kernel, nx, ny),
        out_shape=out_shape,
        in_specs=[smem, smem] + [hbm] * 7,
        out_specs=(vmem, vmem, vmem),
        scratch_shapes=[
            pltpu.VMEM(w_query.shape, BF16),
            pltpu.VMEM((features, 2 * kcols), BF16),
            pltpu.VMEM(w_out.shape, BF16),
            pltpu.VMEM((ny,) + stored_rows.shape, BF16),
            pltpu.VMEM((ny,) + new_rows.shape, BF16),
            pltpu.VMEM((rows, features), BF16),
            pltpu.VMEM((2, ROWS_DEV, slots + PAD, kcols), BF16),
            pltpu.VMEM((rows, qcols), F32),
            pltpu.VMEM((nx, ROWS_DEV, qcols + 2 * kcols), F32),
            pltpu.VMEM((nx, ROWS_DEV, qcols + 2 * kcols), F32),
            pltpu.VMEM((nx, LC, 2 * kcols), F32),
            pltpu.VMEM((nx, LC, 2 * kcols), BF16),
            pltpu.VMEM((nx, LC, 2 * kcols), BF16),
            pltpu.VMEM((nx, ROWS_DEV, qcols), BF16),
            pltpu.VMEM((ny, rows_here, width), BF16),
            pltpu.VMEM((ny, rows_here, width), BF16),
            dma((nq,)), dma((2,)), dma((nq,)), dma((1,)), dma((nst,)), dma((1,)),
            dma((ny,)), dma((ny,)), dma((3, nst)), dma((3, nst)),
            dma((nx,)), dma((nx,)), dma((nx,)), dma((nx,)),
            dma((nx,)), dma((nx,)), dma((ny, halves)), dma((ny, halves)),
        ],
        compiler_params=pltpu.CompilerParams(
            collective_id=0, has_side_effects=True, vmem_limit_bytes=60 * 1024 * 1024
        ),
    )(cache_len, owner, stored_rows, new_rows, w_query, w_key, w_value, w_out, kv_cache)
    return pl.pallas_call(
        hand_over,
        out_shape=out_shape,
        in_specs=[hbm] * 3,
        out_specs=(hbm,) * 3,
        scratch_shapes=[pltpu.VMEM(o.shape, o.dtype) for o in out_shape] + [dma((3,)), dma((3,))],
    )(*results)


def solution(mesh):
    in_specs = (
        P(("groups", "gy"), "gx"),
        P(("groups", "gy"), "gx"),
        P("gx", "gy"),
        P("gx", "gy"),
        P("gx", "gy"),
        P("gy", "gx"),
        P(None, ("groups", "gx"), None, "gy"),
        P(("groups", "gx")),
        P("groups"),
    )
    out_specs = (
        P(("groups", "gy"), "gx"),
        P(("groups", "gx"), None, "gy"),
        P(("groups", "gx"), None, "gy"),
    )
    return jax.shard_map(
        per_device, mesh=mesh, in_specs=in_specs, out_specs=out_specs, check_vma=False
    )
```
